128 devices in a mesh: dp: 4 (over y), expert: 4 (over x), tensor: 8 (over z, core).
Axes of the slice: x: 4, y: 4, z: 4, core: 2. Of those that a mesh axis runs over, the one named last changes fastest.
Arguments:
- tokens: bfloat16 [2048, 6144], P(('dp', 'expert'), 'tensor'), may hold values from -6 to 6
- grad_out: bfloat16 [2048, 6144], P(('dp', 'expert'), 'tensor'), may hold values from -6 to 6
- expert_ids: int32 [2048, 4], P(('dp', 'expert')), may hold values from 0 to 15, all different within a row; in each aligned block of 128 rows (0 to 127, 128 to 255, ...) at most 48 rows name the same one
- gate_fixed: int32 [2048, 4], P(('dp', 'expert')), may hold values from 8192 to 65535
- w_gate: bfloat16 [4, 5376, 6144], P('expert', ('dp', 'tensor')), may hold values from -0.078125 to 0.078125
- w_up: bfloat16 [4, 5376, 6144], P('expert', ('dp', 'tensor')), may hold values from -0.078125 to 0.078125
- w_down: bfloat16 [4, 5376, 6144], P('expert', ('dp', 'tensor')), may hold values from -0.078125 to 0.078125
Outputs:
- mixed: bfloat16 [2048, 6144], P(('dp', 'expert'), 'tensor')
- grad_tokens: bfloat16 [2048, 6144], P(('dp', 'expert'), 'tensor')
- grad_gate: float32 [4, 5376, 6144], P('expert', ('dp', 'tensor'))
- grad_up: float32 [4, 5376, 6144], P('expert', ('dp', 'tensor'))
- grad_down: float32 [4, 5376, 6144], P('expert', ('dp', 'tensor'))
The draws below stay inside these ranges and needn't reach their ends.
Inputs may be any that keep to these rules, and one draw needn't show every extreme that they name: `expert_ids`: each row names 4 different experts; in each aligned block of 128 rows no expert is named by more than 48 rows, a bound that some block reaches.
All inputs are finite; a program needn't handle non-finite values.
Results may differ from the reference program's by a relative error of at most 0.02.
Values may be sent and summed in bfloat16 or wider, within the bound.
No kernel may reach another device: no remote copies, remote signals or barrier semaphores. Data moves between devices by JAX's collectives and lax.ppermute only.
A program may use at most 128 MiB of HBM per device.

```python
import math
import jax
import jax.numpy as jnp
import numpy as np
from jax import lax

D = 6144
FFW = 5376
E = 16
TOPK = 4
TOK_DEV = 128
CAP = 48
TOKENS = 2048
N_DP = 4
N_EXPERT = 4
N_TENSOR = 8


def touch_ends(entries, own_key, low, top_value):
    spot = [jax.random.randint(jax.random.fold_in(own_key, axis), (), 0, length) for axis, length in enumerate(entries.shape)]
    longest = entries.shape.index(max(entries.shape))
    next_to = spot[:longest] + [(spot[longest] + 1) % entries.shape[longest]] + spot[longest + 1:]
    return entries.at[tuple(spot)].set(low).at[tuple(next_to)].set(top_value)


def block_scale(own_key, shape, cuts, low, high):
    loudness, own = 1.0, jax.random.fold_in(own_key, 6)
    for dim, parts in cuts:
        steps = jnp.exp(jax.random.uniform(jax.random.fold_in(own, dim), (parts,), jnp.float32, low / len(cuts), high / len(cuts)))
        loudness = loudness * jnp.repeat(steps, shape[dim] // parts).reshape([-1 if axis == dim else 1 for axis in range(len(shape))])
    return loudness


def shared_out(key, own, number, rows, amount, top, reach, skew):
    order = jax.random.permutation(key, amount)
    crowded, ordinary = load_shares(amount, rows * top, reach, skew, True), load_shares(amount, rows * top, reach, skew, False)
    places = jnp.arange(amount)

    def named(tallies, offset_by):
        used = int((tallies > 0).sum())
        fixed = max(1, used // 4)
        moved = fixed + (places - fixed + offset_by * (used - fixed)) % max(1, amount - fixed)
        return jnp.zeros((amount,), jnp.int32).at[order[jnp.where(places < fixed, places, moved)]].set(jnp.asarray(tallies, jnp.int32))

    tallies = jnp.where(number % 4 == 0, named(crowded, number // 4), named(ordinary, number - number // 4 - 1))
    mixed = jax.random.permutation(jax.random.fold_in(own, 3), amount)
    source_of, sink = mixed[0:amount // 2 * 2:2], mixed[1:amount // 2 * 2:2]
    margin = jnp.minimum(tallies[source_of] - 1, reach - tallies[sink]) // 2
    margin = jnp.where((source_of == order[0]) | (sink == order[0]) | (tallies[sink] == 0), 0, jnp.maximum(margin, 0))
    moved = jax.random.randint(jax.random.fold_in(own, 4), (amount // 2,), 0, 1 << 20) % (margin + 1)
    tallies = tallies.at[source_of].add(-moved).at[sink].add(moved)
    items = jnp.searchsorted(jnp.cumsum(tallies), jnp.arange(rows * top), side="right").astype(jnp.int32)
    listing = items.reshape(top, rows).T
    listing = listing[jax.random.permutation(jax.random.fold_in(own, 1), rows)]
    offset_by = jax.random.randint(jax.random.fold_in(own, 2), (rows, 1), 0, top)
    return jnp.take_along_axis(listing, (jnp.arange(top)[None, :] + offset_by) % top, axis=1)


def load_shares(count, total, most, skew, full):
    portions = [(1 << 20) // math.isqrt(rank ** skew) + 1 for rank in range(1, count + 1)]
    largest = most if full else min(most, max(-(-total // count), total * portions[0] // sum(portions)))
    least = 1 if total - largest >= count - 1 else 0
    given, rest = [largest] + [least] * (count - 1), total - largest - least * (count - 1)
    while rest > 0:
        movable = [i for i in range(1, count) if given[i] < largest] or [i for i in range(1, count) if given[i] < most]
        pool, remaining = sum([portions[i] for i in movable]), rest
        for i in movable:
            extra = min(most - given[i], max(1, remaining * portions[i] // pool), rest)
            given[i] = given[i] + extra
            rest = rest - extra
    return np.array(given)


def gaussian(key, shape, deviation, most, pieces=(), held_as=jnp.bfloat16):
    level = block_scale(key, shape, pieces, -0.22, 0.18) if pieces else 1.0
    array = jax.random.normal(key, shape, jnp.float32) * deviation * level
    return jnp.minimum(jnp.maximum(array, -most), most).astype(held_as)


def setup_inputs(seed: int = 0) -> dict:
    arg_keys = jax.random.split(jax.random.key(seed), 8)
    tokens = gaussian(arg_keys[0], (TOKENS, D), 1.0, 6.0, ((0, 16), (1, 8)))
    grad_out = gaussian(arg_keys[1], (TOKENS, D), 1.0, 6.0, ((0, 16), (1, 8)))
    expert_ids_keys = jax.random.split(jax.random.fold_in(arg_keys[2], 1), TOKENS // TOK_DEV)
    expert_ids_turns = jax.random.permutation(jax.random.fold_in(arg_keys[2], 3), TOKENS // TOK_DEV)
    expert_ids = jax.vmap(lambda own, number: shared_out(jax.random.fold_in(arg_keys[2], 2), own, number, TOK_DEV, E, TOPK, CAP, 2))(expert_ids_keys, expert_ids_turns).reshape((TOKENS, TOPK))
    gate_fixed = touch_ends(jax.random.randint(arg_keys[3], (TOKENS, TOPK), 8192, 65536), jax.random.fold_in(arg_keys[3], 1), 8192, 65535).astype(jnp.int32)
    w_gate = gaussian(arg_keys[4], (N_EXPERT, FFW, D), D ** -0.5, 0.078125, ((0, 4), (1, 32)))
    w_up = gaussian(arg_keys[5], (N_EXPERT, FFW, D), D ** -0.5, 0.078125, ((0, 4), (1, 32)))
    w_down = gaussian(arg_keys[6], (N_EXPERT, FFW, D), FFW ** -0.5, 0.078125, ((0, 4), (1, 32)))
    return {"tokens": tokens, "grad_out": grad_out, "expert_ids": expert_ids, "gate_fixed": gate_fixed, "w_gate": w_gate, "w_up": w_up, "w_down": w_down}


def slot_tables(expert_ids, gate_fixed):
    gate_value = gate_fixed.astype(jnp.float32) * (1.0 / 65536.0)
    matches = expert_ids[:, :, None] == jnp.arange(N_EXPERT, dtype=jnp.int32)[None, None, :]
    chosen = jnp.any(matches, axis=1).astype(jnp.int32)
    weight = jnp.sum(jnp.where(matches, gate_value[:, :, None], 0.0), axis=1)
    slot_rank = jnp.cumsum(chosen, axis=0) - chosen
    in_slot = (slot_rank[:, :, None] == jnp.arange(CAP, dtype=jnp.int32)[None, None, :]) & (chosen[:, :, None] > 0)
    slot_table = jnp.transpose(in_slot.astype(jnp.float32), (1, 2, 0))
    slot_gate = jnp.einsum("jct,tj->jc", slot_table, weight, precision=lax.Precision.HIGHEST)
    return slot_table, slot_gate


def reference(tokens, grad_out, expert_ids, gate_fixed, w_gate, w_up, w_down):
    groups = TOKENS // TOK_DEV
    tok_groups = tokens.reshape(groups, TOK_DEV, D).astype(jnp.float32)
    cot_groups = grad_out.reshape(groups, TOK_DEV, D).astype(jnp.float32)
    slot_table, slot_gate = jax.vmap(slot_tables)(expert_ids.reshape(groups, TOK_DEV, TOPK), gate_fixed.reshape(groups, TOK_DEV, TOPK))
    slot_rows = jnp.einsum("gjct,gtf->gjcf", slot_table, tok_groups, precision=lax.Precision.HIGHEST).astype(jnp.bfloat16)
    slot_cots = (jnp.einsum("gjct,gtf->gjcf", slot_table, cot_groups, precision=lax.Precision.HIGHEST) * slot_gate[:, :, :, None]).astype(jnp.bfloat16)
    panel_count = N_DP * N_TENSOR
    panel_width = FFW // panel_count
    outs_list, backs_list, grads_gate, grads_up, grads_down = [], [], [], [], []
    for expert_index in range(N_EXPERT):
        row_feats = slot_rows[:, expert_index].reshape(groups * CAP, D)
        row_cots = slot_cots[:, expert_index].reshape(groups * CAP, D)
        gate_mat = w_gate[expert_index]
        up_mat = w_up[expert_index]
        down_mat = w_down[expert_index]
        gate_pre = lax.dot_general(row_feats, gate_mat, (((1,), (1,)), ((), ())), preferred_element_type=jnp.float32)
        up_pre = lax.dot_general(row_feats, up_mat, (((1,), (1,)), ((), ())), preferred_element_type=jnp.float32)
        gate_sig = jax.nn.sigmoid(gate_pre)
        hidden = (gate_pre * gate_sig * up_pre).astype(jnp.bfloat16)
        hid_grad = lax.dot_general(row_cots, down_mat, (((1,), (1,)), ((), ())), preferred_element_type=jnp.float32)
        d_gate = (hid_grad * up_pre * gate_sig * (1.0 + gate_pre * (1.0 - gate_sig))).astype(jnp.bfloat16)
        d_up = (hid_grad * gate_pre * gate_sig).astype(jnp.bfloat16)
        grads_gate.append(lax.dot_general(d_gate, row_feats, (((0,), (0,)), ((), ())), preferred_element_type=jnp.float32))
        grads_up.append(lax.dot_general(d_up, row_feats, (((0,), (0,)), ((), ())), preferred_element_type=jnp.float32))
        grads_down.append(lax.dot_general(hidden, row_cots, (((0,), (0,)), ((), ())), preferred_element_type=jnp.float32))

        def add_panel(totals, panel_index):
            out_total, back_total = totals
            column = panel_index * panel_width
            hid_panel = lax.dynamic_slice_in_dim(hidden, column, panel_width, 1)
            dg_panel = lax.dynamic_slice_in_dim(d_gate, column, panel_width, 1)
            du_panel = lax.dynamic_slice_in_dim(d_up, column, panel_width, 1)
            down_panel = lax.dynamic_slice_in_dim(down_mat, column, panel_width, 0)
            gate_panel = lax.dynamic_slice_in_dim(gate_mat, column, panel_width, 0)
            up_panel = lax.dynamic_slice_in_dim(up_mat, column, panel_width, 0)
            out_part = jnp.dot(hid_panel, down_panel, preferred_element_type=jnp.float32)
            back_part = jnp.dot(dg_panel, gate_panel, preferred_element_type=jnp.float32)
            back_part = back_part + jnp.dot(du_panel, up_panel, preferred_element_type=jnp.float32)
            out_total = out_total + lax.optimization_barrier(out_part.astype(jnp.bfloat16)).astype(jnp.float32)
            back_total = back_total + lax.optimization_barrier(back_part.astype(jnp.bfloat16)).astype(jnp.float32)
            return (out_total, back_total), None

        zeros_rows = jnp.zeros((groups * CAP, D), jnp.float32)
        (out_total, back_total), _ = lax.scan(add_panel, (zeros_rows, zeros_rows), jnp.arange(panel_count, dtype=jnp.int32))
        outs_list.append(out_total.astype(jnp.bfloat16).reshape(groups, CAP, D))
        backs_list.append(back_total.astype(jnp.bfloat16).reshape(groups, CAP, D))
    expert_out = jnp.stack(outs_list, axis=1).astype(jnp.float32) * slot_gate[:, :, :, None]
    expert_back = jnp.stack(backs_list, axis=1).astype(jnp.float32)
    mixed = jnp.einsum("gjct,gjcf->gtf", slot_table, expert_out, precision=lax.Precision.HIGHEST)
    grad_tokens = jnp.einsum("gjct,gjcf->gtf", slot_table, expert_back, precision=lax.Precision.HIGHEST)
    mixed = mixed.reshape(TOKENS, D).astype(jnp.bfloat16)
    grad_tokens = grad_tokens.reshape(TOKENS, D).astype(jnp.bfloat16)
    return mixed, grad_tokens, jnp.stack(grads_gate, axis=0), jnp.stack(grads_up, axis=0), jnp.stack(grads_down, axis=0)
```

```python
import jax
import jax.numpy as jnp
from jax import lax
from jax.experimental import pallas as pl
from jax.experimental.pallas import tpu as pltpu
from jax.sharding import Mesh
from jax.sharding import PartitionSpec as P

CAP = 48
VMEM_LIMIT = 48 * 1024 * 1024
PLANE = ("dp", "z")
SWAP = [(0, 1), (1, 0)]


def slot_tables(expert_ids, gate_fixed, expert_count):
    gate_value = gate_fixed.astype(jnp.float32) * (1.0 / 65536.0)
    matches = expert_ids[:, :, None] == jnp.arange(expert_count, dtype=jnp.int32)[None, None, :]
    chosen = jnp.any(matches, axis=1).astype(jnp.int32)
    weight = jnp.sum(jnp.where(matches, gate_value[:, :, None], 0.0), axis=1)
    slot_rank = jnp.cumsum(chosen, axis=0) - chosen
    in_slot = (slot_rank[:, :, None] == jnp.arange(CAP, dtype=jnp.int32)[None, None, :]) & (
        chosen[:, :, None] > 0
    )
    slot_table = jnp.transpose(in_slot.astype(jnp.float32), (1, 2, 0))
    slot_gate = jnp.einsum("jct,tj->jc", slot_table, weight, precision=lax.Precision.HIGHEST)
    return (slot_table, slot_gate)


def dot(a, b, dims):
    return lax.dot_general(a, b, (dims, ((), ())), preferred_element_type=jnp.float32)


def params(semantics=("arbitrary",)):
    return pltpu.CompilerParams(dimension_semantics=semantics, vmem_limit_bytes=VMEM_LIMIT)


def pack_columns(core, w_gate, w_up, w_down, z_count, width):
    hidden = w_gate.shape[1]

    def kernel(core_ref, g_ref, u_ref, d_ref, out_ref):
        out_ref[0, 0] = g_ref[0]
        out_ref[1, 0] = u_ref[0]
        out_ref[2, 0] = d_ref[0]

    spec = pl.BlockSpec((1, hidden, width), lambda z, core_ref: (0, 0, 2 * z + 1 - core_ref[0]))
    return pl.pallas_call(
        kernel,
        out_shape=jax.ShapeDtypeStruct((3, z_count, hidden, width), w_gate.dtype),
        grid_spec=pltpu.PrefetchScalarGridSpec(
            num_scalar_prefetch=1,
            grid=(z_count,),
            in_specs=[spec, spec, spec],
            out_specs=pl.BlockSpec((3, 1, hidden, width), lambda z, core_ref: (0, z, 0, 0)),
        ),
        compiler_params=params(),
        cost_estimate=pl.CostEstimate(
            flops=0, bytes_accessed=12 * z_count * hidden * width, transcendentals=0
        ),
        name="pack_columns",
    )(core, w_gate, w_up, w_down)


def forward(gathered, w_gate, w_up, w_down):
    dp, tensor, _, slots, width = gathered.shape
    rows = dp * slots
    hidden = w_gate.shape[1]

    def kernel(x_ref, g_ref, u_ref, d_ref, out_ref, gate_acc, up_acc, dhid_acc):
        t = pl.program_id(0)
        toks = x_ref[:, 0, 0].reshape(rows, width)
        cots = x_ref[:, 0, 1].reshape(rows, width)
        last = ((1,), (1,))
        gate_part = dot(g_ref[0], toks, last)
        up_part = dot(u_ref[0], toks, last)
        dhid_part = dot(d_ref[0], cots, last)

        @pl.when(t == 0)
        def _():
            gate_acc[...] = gate_part
            up_acc[...] = up_part
            dhid_acc[...] = dhid_part

        @pl.when(t > 0)
        def _():
            gate_acc[...] += gate_part
            up_acc[...] += up_part
            dhid_acc[...] += dhid_part

        @pl.when(t == tensor - 1)
        def _():
            gate = gate_acc[...]
            up = up_acc[...]
            dhid = dhid_acc[...]
            sig = jax.nn.sigmoid(gate)
            out_ref[0] = (gate * sig * up).astype(out_ref.dtype)
            out_ref[1] = (dhid * up * sig * (1.0 + gate * (1.0 - sig))).astype(out_ref.dtype)
            out_ref[2] = (dhid * gate * sig).astype(out_ref.dtype)

    w_spec = pl.BlockSpec((1, hidden, width), lambda t: (0, 0, t))
    return pl.pallas_call(
        kernel,
        out_shape=jax.ShapeDtypeStruct((3, hidden, rows), gathered.dtype),
        grid=(tensor,),
        in_specs=[
            pl.BlockSpec((dp, 1, 2, slots, width), lambda t: (0, t, 0, 0, 0)),
            w_spec,
            w_spec,
            w_spec,
        ],
        out_specs=pl.BlockSpec((3, hidden, rows), lambda t: (0, 0, 0)),
        scratch_shapes=[pltpu.VMEM((hidden, rows), jnp.float32)] * 3,
        compiler_params=params(),
        cost_estimate=pl.CostEstimate(
            flops=6 * rows * hidden * width * tensor,
            bytes_accessed=(4 * rows + 6 * hidden) * width * tensor,
            transcendentals=rows * hidden,
        ),
        name="forward",
    )(gathered, w_gate, w_up, w_down)


def block_products(core, mine, other, w_gate, w_up, w_down, other_cols, dp):
    _, hidden, rows = mine.shape
    _, z_count, _, width = other_cols.shape
    slots = rows // dp

    def kernel(core_ref, mt_ref, ot_ref, g_ref, u_ref, d_ref, oc_ref, out_ref, m_ref, o_ref):
        inner = ((1,), (0,))

        @pl.when(pl.program_id(0) == 0)
        def _():
            for k in range(3):
                m_ref[k] = mt_ref[k].T
                o_ref[k] = ot_ref[k].T

        out = dot(m_ref[0], d_ref[0], inner) + dot(o_ref[0], oc_ref[2, 0], inner)
        out_ref[:, 0, :, :width] = out.astype(out_ref.dtype).reshape(dp, slots, width)
        back = dot(m_ref[1], g_ref[0], inner) + dot(o_ref[1], oc_ref[0, 0], inner)
        back = back + dot(m_ref[2], u_ref[0], inner) + dot(o_ref[2], oc_ref[1, 0], inner)
        out_ref[:, 0, :, width:] = back.astype(out_ref.dtype).reshape(dp, slots, width)

    acts = pl.BlockSpec((3, hidden, rows), lambda z, core_ref: (0, 0, 0))
    cols = pl.BlockSpec((1, hidden, width), lambda z, core_ref: (0, 0, 2 * z + core_ref[0]))
    return pl.pallas_call(
        kernel,
        out_shape=jax.ShapeDtypeStruct((dp, z_count, slots, 2 * width), mine.dtype),
        grid_spec=pltpu.PrefetchScalarGridSpec(
            num_scalar_prefetch=1,
            grid=(z_count,),
            in_specs=[
                acts,
                acts,
                cols,
                cols,
                cols,
                pl.BlockSpec((3, 1, hidden, width), lambda z, core_ref: (0, z, 0, 0)),
            ],
            out_specs=pl.BlockSpec(
                (dp, 1, slots, 2 * width), lambda z, core_ref: (0, z, 0, 0)
            ),
            scratch_shapes=[pltpu.VMEM((3, rows, hidden), mine.dtype)] * 2,
        ),
        compiler_params=params(),
        cost_estimate=pl.CostEstimate(
            flops=12 * rows * hidden * width * z_count,
            bytes_accessed=(4 * rows + 12 * hidden) * width * z_count,
            transcendentals=0,
        ),
        name="block_products",
    )(core, mine, other, w_gate, w_up, w_down, other_cols)


def weight_grads(acts_t, gathered):
    dp, tensor, _, slots, width = gathered.shape
    _, hidden, rows = acts_t.shape

    def kernel(a_ref, x_ref, g_ref, u_ref, d_ref):
        toks = x_ref[:, 0, 0].reshape(rows, width)
        cots = x_ref[:, 0, 1].reshape(rows, width)
        inner = ((1,), (0,))
        g_ref[0] = dot(a_ref[1], toks, inner)
        u_ref[0] = dot(a_ref[2], toks, inner)
        d_ref[0] = dot(a_ref[0], cots, inner)

    out = jax.ShapeDtypeStruct((1, hidden, tensor * width), jnp.float32)
    o_spec = pl.BlockSpec((1, hidden, width), lambda t: (0, 0, t))
    return pl.pallas_call(
        kernel,
        out_shape=(out, out, out),
        grid=(tensor,),
        in_specs=[
            pl.BlockSpec((3, hidden, rows), lambda t: (0, 0, 0)),
            pl.BlockSpec((dp, 1, 2, slots, width), lambda t: (0, t, 0, 0, 0)),
        ],
        out_specs=(o_spec, o_spec, o_spec),
        compiler_params=params(),
        cost_estimate=pl.CostEstimate(
            flops=6 * rows * hidden * width * tensor,
            bytes_accessed=(4 * rows + 12 * hidden) * width * tensor,
            transcendentals=0,
        ),
        name="weight_grads",
    )(acts_t, gathered)


def on_device(tokens, grad_out, expert_ids, gate_fixed, w_gate, w_up, w_down):
    expert_count = lax.axis_size("expert")
    dp_count = lax.axis_size("dp")
    z_count = lax.axis_size("z")
    width = tokens.shape[1]
    core = lax.axis_index("core").astype(jnp.int32).reshape(1)
    slot_table, slot_gate = slot_tables(expert_ids, gate_fixed, expert_count)
    table_half = slot_table.astype(jnp.bfloat16)
    send_rows = jnp.einsum(
        "jct,tf->jcf", table_half, tokens, preferred_element_type=jnp.float32
    ).astype(jnp.bfloat16)
    send_cots = jnp.einsum("jct,tf->jcf", table_half, grad_out, preferred_element_type=jnp.float32)
    send_cots = (send_cots * slot_gate[:, :, None]).astype(jnp.bfloat16)
    got = lax.all_to_all(
        jnp.concatenate([send_rows, send_cots], axis=1),
        "expert",
        split_axis=0,
        concat_axis=0,
        tiled=True,
    )
    slots = expert_count * CAP
    shard = jnp.concatenate(
        [got[:, :CAP].reshape(slots, width), got[:, CAP:].reshape(slots, width)], axis=0
    )
    core, shard = lax.optimization_barrier((core, shard))
    gathered = lax.all_gather(shard, ("dp", "z", "core"), axis=0, tiled=True)
    gathered = gathered.reshape(dp_count, z_count * 2, 2, slots, width)
    packed = pack_columns(core, w_gate, w_up, w_down, z_count, width)
    other_cols = lax.ppermute(packed, "core", SWAP)
    mine = forward(gathered, w_gate, w_up, w_down)
    other = lax.ppermute(mine, "core", SWAP)
    terms = block_products(core, mine, other, w_gate, w_up, w_down, other_cols, dp_count)
    summed = lax.psum_scatter(
        terms.reshape(dp_count * z_count * slots, 2 * width),
        PLANE,
        scatter_dimension=0,
        tiled=True,
    )
    grad_g, grad_u, grad_d = weight_grads(mine, gathered)
    summed, grad_g, grad_u, grad_d = lax.optimization_barrier((summed, grad_g, grad_u, grad_d))
    summed = summed.reshape(expert_count, CAP, 2 * width)
    returned = lax.all_to_all(summed, "expert", split_axis=0, concat_axis=0, tiled=True)
    expert_out = returned[:, :, :width].astype(jnp.float32) * slot_gate[:, :, None]
    expert_back = returned[:, :, width:].astype(jnp.float32)
    mixed = jnp.einsum(
        "jct,jcf->tf", slot_table, expert_out, precision=lax.Precision.HIGHEST
    ).astype(jnp.bfloat16)
    grad_tokens = jnp.einsum(
        "jct,jcf->tf", slot_table, expert_back, precision=lax.Precision.HIGHEST
    ).astype(jnp.bfloat16)
    return (mixed, grad_tokens, grad_g, grad_u, grad_d)


def solution(mesh):
    dp, expert, tensor = (mesh.shape[a] for a in ("dp", "expert", "tensor"))
    fine = Mesh(mesh.devices.reshape(dp, expert, tensor // 2, 2), ("dp", "expert", "z", "core"))
    feats = P(("dp", "expert"), ("z", "core"))
    ids = P(("dp", "expert"), None)
    weights = P("expert", ("dp", "z", "core"), None)
    return jax.shard_map(
        on_device,
        mesh=fine,
        in_specs=(feats, feats, ids, ids, weights, weights, weights),
        out_specs=(feats, feats, weights, weights, weights),
        check_vma=False,
    )
```

```python
import jax
import jax.numpy as jnp
from jax import lax
from jax.experimental import pallas as pl
from jax.experimental.pallas import tpu as pltpu
from jax.sharding import Mesh
from jax.sharding import PartitionSpec as P

CAP = 48
VMEM_LIMIT = 61 * 1024 * 1024
RING = 4
SWAP = [(0, 1), (1, 0)]


def slot_tables(expert_ids, gate_fixed, expert_count):
    gate_value = gate_fixed.astype(jnp.float32) * (1.0 / 65536.0)
    matches = expert_ids[:, :, None] == jnp.arange(expert_count, dtype=jnp.int32)[None, None, :]
    chosen = jnp.any(matches, axis=1).astype(jnp.int32)
    weight = jnp.sum(jnp.where(matches, gate_value[:, :, None], 0.0), axis=1)
    slot_rank = jnp.cumsum(chosen, axis=0) - chosen
    in_slot = (slot_rank[:, :, None] == jnp.arange(CAP, dtype=jnp.int32)[None, None, :]) & (
        chosen[:, :, None] > 0
    )
    slot_table = jnp.transpose(in_slot.astype(jnp.float32), (1, 2, 0))
    slot_gate = jnp.einsum("jct,tj->jc", slot_table, weight, precision=lax.Precision.HIGHEST)
    return (slot_table, slot_gate)


def turned(index, by):
    return (index + by) & (RING - 1)


def dot(a, b, dims):
    return lax.dot_general(a, b, (dims, ((), ())), preferred_element_type=jnp.float32)


def params(semantics=("arbitrary",)):
    return pltpu.CompilerParams(dimension_semantics=semantics, vmem_limit_bytes=VMEM_LIMIT)


def pack_columns(place, w_gate, w_up, w_down, z_count, width):
    hidden = w_gate.shape[1]

    def kernel(core_ref, g_ref, u_ref, d_ref, out_ref):
        out_ref[0, 0] = g_ref[0]
        out_ref[1, 0] = u_ref[0]
        out_ref[2, 0] = d_ref[0]

    spec = pl.BlockSpec((1, hidden, width), lambda z, core_ref: (0, 0, 2 * z + 1 - core_ref[0]))
    return pl.pallas_call(
        kernel,
        out_shape=jax.ShapeDtypeStruct((3, z_count, hidden, width), w_gate.dtype),
        grid_spec=pltpu.PrefetchScalarGridSpec(
            num_scalar_prefetch=1,
            grid=(z_count,),
            in_specs=[spec, spec, spec],
            out_specs=pl.BlockSpec((3, 1, hidden, width), lambda z, core_ref: (0, z, 0, 0)),
        ),
        compiler_params=params(),
        cost_estimate=pl.CostEstimate(
            flops=0, bytes_accessed=12 * z_count * hidden * width, transcendentals=0
        ),
        name="pack_columns",
    )(place, w_gate, w_up, w_down)


def forward(gathered, w_gate, w_up, w_down):
    dp, tensor, _, slots, width = gathered.shape
    rows = dp * slots
    hidden = w_gate.shape[1]

    def kernel(x_ref, g_ref, u_ref, d_ref, out_ref, gate_acc, up_acc, dhid_acc):
        t = pl.program_id(0)
        toks = x_ref[:, 0, 0].reshape(rows, width)
        cots = x_ref[:, 0, 1].reshape(rows, width)
        last = ((1,), (1,))
        gate_part = dot(g_ref[0], toks, last)
        up_part = dot(u_ref[0], toks, last)
        dhid_part = dot(d_ref[0], cots, last)

        @pl.when(t == 0)
        def _():
            gate_acc[...] = gate_part
            up_acc[...] = up_part
            dhid_acc[...] = dhid_part

        @pl.when(t > 0)
        def _():
            gate_acc[...] += gate_part
            up_acc[...] += up_part
            dhid_acc[...] += dhid_part

        @pl.when(t == tensor - 1)
        def _():
            gate = gate_acc[...]
            up = up_acc[...]
            dhid = dhid_acc[...]
            sig = jax.nn.sigmoid(gate)
            out_ref[0] = (gate * sig * up).astype(out_ref.dtype)
            out_ref[1] = (dhid * up * sig * (1.0 + gate * (1.0 - sig))).astype(out_ref.dtype)
            out_ref[2] = (dhid * gate * sig).astype(out_ref.dtype)

    w_spec = pl.BlockSpec((1, hidden, width), lambda t: (0, 0, t))
    return pl.pallas_call(
        kernel,
        out_shape=jax.ShapeDtypeStruct((3, hidden, rows), gathered.dtype),
        grid=(tensor,),
        in_specs=[
            pl.BlockSpec((dp, 1, 2, slots, width), lambda t: (0, t, 0, 0, 0)),
            w_spec,
            w_spec,
            w_spec,
        ],
        out_specs=pl.BlockSpec((3, hidden, rows), lambda t: (0, 0, 0)),
        scratch_shapes=[pltpu.VMEM((hidden, rows), jnp.float32)] * 3,
        compiler_params=params(),
        cost_estimate=pl.CostEstimate(
            flops=6 * rows * hidden * width * tensor,
            bytes_accessed=(4 * rows + 6 * hidden) * width * tensor,
            transcendentals=rows * hidden,
        ),
        name="forward",
    )(gathered, w_gate, w_up, w_down)


def out_terms(place, mine, other, w_down, other_cols, dp, shifts):
    _, hidden, rows = mine.shape
    _, z_count, _, width = other_cols.shape
    slots = rows // dp
    count = len(shifts)

    def kernel(place_ref, mt_ref, ot_ref, d_ref, oc_ref, *refs):
        *out_refs, flip_ref, m_ref, o_ref = refs
        z = pl.program_id(0)

        @pl.when(z == 0)
        def _():
            for src, dst in ((mt_ref, m_ref), (ot_ref, o_ref)):
                flip_ref[...] = src[0].T
                for k, shift in enumerate(shifts):
                    block = turned(place_ref[1], shift)
                    start = pl.multiple_of(block * slots, slots)
                    dst[k * slots : (k + 1) * slots] = flip_ref[pl.ds(start, slots)]

        inner = ((1,), (0,))
        out = dot(m_ref[...], d_ref[0], inner) + dot(o_ref[...], oc_ref[0, 0], inner)
        out = out.astype(mine.dtype).reshape(count, slots, width)
        if count > 1:
            for k in range(count):
                out_refs[k][0] = out[k]
            return

        @pl.when(z < 2)
        def _():
            out_refs[0][z] = out[0]

        @pl.when(z >= 2)
        def _():
            out_refs[1][z - 2] = out[0]

    acts = pl.BlockSpec((1, hidden, rows), lambda z, place_ref: (0, 0, 0))
    whole = pl.BlockSpec((2, slots, width), lambda z, place_ref: (0, 0, 0))
    step = pl.BlockSpec((1, slots, width), lambda z, place_ref: (z, 0, 0))
    halves = jax.ShapeDtypeStruct((2, slots, width), mine.dtype)
    blocks = jax.ShapeDtypeStruct((z_count, slots, width), mine.dtype)
    return pl.pallas_call(
        kernel,
        out_shape=[blocks] * count if count > 1 else [halves] * 2,
        grid_spec=pltpu.PrefetchScalarGridSpec(
            num_scalar_prefetch=1,
            grid=(z_count,),
            in_specs=[
                acts,
                acts,
                pl.BlockSpec((1, hidden, width), lambda z, place_ref: (0, 0, 2 * z + place_ref[0])),
                pl.BlockSpec((1, 1, hidden, width), lambda z, place_ref: (2, z, 0, 0)),
            ],
            out_specs=[step] * count if count > 1 else [whole] * 2,
            scratch_shapes=[
                pltpu.VMEM((rows, hidden), mine.dtype),
                pltpu.VMEM((count * slots, hidden), mine.dtype),
                pltpu.VMEM((count * slots, hidden), mine.dtype),
            ],
        ),
        compiler_params=params(),
        cost_estimate=pl.CostEstimate(
            flops=4 * count * slots * hidden * width * z_count,
            bytes_accessed=(2 * count * slots + 4 * hidden) * width * z_count,
            transcendentals=0,
        ),
        name="out_terms",
    )(place, mine, other, w_down, other_cols)


def back_terms(place, mine, other, w_gate, w_up, other_cols, dp, shifts):
    _, hidden, rows = mine.shape
    _, z_count, _, width = other_cols.shape
    slots = rows // dp
    count = len(shifts)
    blocks = jnp.stack([turned(place[2], shift) for shift in shifts])
    place = jnp.concatenate([place[:1], blocks])

    def kernel(place_ref, mt_ref, ot_ref, g_ref, u_ref, oc_ref, *refs):
        *out_refs, m_ref, o_ref = refs
        j = pl.program_id(0)

        @pl.when(j == 0)
        def _():
            for k in range(2):
                m_ref[k] = mt_ref[k + 1].T
                o_ref[k] = ot_ref[k + 1].T

        inner = ((1,), (0,))
        back = dot(m_ref[0], g_ref[0], inner) + dot(o_ref[0], oc_ref[0, 0], inner)
        back = back + dot(m_ref[1], u_ref[0], inner) + dot(o_ref[1], oc_ref[1, 0], inner)
        back = back.astype(mine.dtype).reshape(dp, slots, width)
        if count == 1:
            out_refs[0][...] = back[: dp // 2]
            out_refs[1][...] = back[dp // 2 :]
        for k in range(count if count > 1 else 0):

            @pl.when(j == k)
            def _(k=k):
                out_refs[k][...] = back


    outs = [dp] * count if count > 1 else [dp // 2] * 2
    acts = pl.BlockSpec((3, hidden, rows), lambda j, place_ref: (0, 0, 0))
    cols = pl.BlockSpec(
        (1, hidden, width), lambda j, place_ref: (0, 0, 2 * place_ref[1 + j] + place_ref[0])
    )
    return pl.pallas_call(
        kernel,
        out_shape=[jax.ShapeDtypeStruct((n, slots, width), mine.dtype) for n in outs],
        grid_spec=pltpu.PrefetchScalarGridSpec(
            num_scalar_prefetch=1,
            grid=(count,),
            in_specs=[
                acts,
                acts,
                cols,
                cols,
                pl.BlockSpec(
                    (2, 1, hidden, width), lambda j, place_ref: (0, place_ref[1 + j], 0, 0)
                ),
            ],
            out_specs=[
                pl.BlockSpec((n, slots, width), lambda j, place_ref: (0, 0, 0)) for n in outs
            ],
            scratch_shapes=[pltpu.VMEM((2, rows, hidden), mine.dtype)] * 2,
        ),
        compiler_params=params(),
        cost_estimate=pl.CostEstimate(
            flops=8 * rows * hidden * width * count,
            bytes_accessed=(2 * rows + 8 * hidden) * width * count,
            transcendentals=0,
        ),
        name="back_terms",
    )(place, mine, other, w_gate, w_up, other_cols)


def wide(x):
    return x.astype(jnp.float32)


def around(axis, by):
    n = lax.axis_size(axis)
    return [(i, (i + by) % n) for i in range(n)]


def add_to_part(x, part, upper):
    free = x.shape[0] - part.shape[0]
    edges = [(free, 0) if upper else (0, free)] + [(0, 0)] * (x.ndim - 1)
    return (wide(x) + jnp.pad(wide(part), edges)).astype(x.dtype)


def first_hop(low, high, axis):
    return (
        lax.ppermute(low, axis, around(axis, 1)),
        lax.ppermute(high, axis, around(axis, -1)),
    )


def second_hop(passing, ahead, behind, axis):
    from_behind, from_ahead = passing
    return (
        lax.ppermute(add_to_part(ahead, from_behind, False), axis, around(axis, 1)),
        lax.ppermute(add_to_part(behind, from_ahead, True), axis, around(axis, -1)),
    )


def picked(own, got, place):
    def at(shift):
        def one(x):
            return wide(lax.dynamic_index_in_dim(x, turned(place, shift), 0, keepdims=False))

        return one(own) + one(got[0]) + one(got[1])

    return at


def weight_grads(acts_t, gathered):
    dp, tensor, _, slots, width = gathered.shape
    _, hidden, rows = acts_t.shape

    def kernel(a_ref, x_ref, g_ref, u_ref, d_ref):
        toks = x_ref[:, 0, 0].reshape(rows, width)
        cots = x_ref[:, 0, 1].reshape(rows, width)
        inner = ((1,), (0,))
        g_ref[0] = dot(a_ref[1], toks, inner)
        u_ref[0] = dot(a_ref[2], toks, inner)
        d_ref[0] = dot(a_ref[0], cots, inner)

    out = jax.ShapeDtypeStruct((1, hidden, tensor * width), jnp.float32)
    o_spec = pl.BlockSpec((1, hidden, width), lambda t: (0, 0, t))
    return pl.pallas_call(
        kernel,
        out_shape=(out, out, out),
        grid=(tensor,),
        in_specs=[
            pl.BlockSpec((3, hidden, rows), lambda t: (0, 0, 0)),
            pl.BlockSpec((dp, 1, 2, slots, width), lambda t: (0, t, 0, 0, 0)),
        ],
        out_specs=(o_spec, o_spec, o_spec),
        compiler_params=params(),
        cost_estimate=pl.CostEstimate(
            flops=6 * rows * hidden * width * tensor,
            bytes_accessed=(4 * rows + 12 * hidden) * width * tensor,
            transcendentals=0,
        ),
        name="weight_grads",
    )(acts_t, gathered)


def on_device(tokens, grad_out, expert_ids, gate_fixed, w_gate, w_up, w_down):
    expert_count = lax.axis_size("expert")
    dp_count = lax.axis_size("dp")
    z_count = lax.axis_size("z")
    width = tokens.shape[1]
    place = jnp.stack([lax.axis_index(a).astype(jnp.int32) for a in ("core", "dp", "z")])
    slot_table, slot_gate = slot_tables(expert_ids, gate_fixed, expert_count)
    table_half = slot_table.astype(jnp.bfloat16)
    send_rows = jnp.einsum(
        "jct,tf->jcf", table_half, tokens, preferred_element_type=jnp.float32
    ).astype(jnp.bfloat16)
    send_cots = jnp.einsum("jct,tf->jcf", table_half, grad_out, preferred_element_type=jnp.float32)
    send_cots = (send_cots * slot_gate[:, :, None]).astype(jnp.bfloat16)
    got = lax.all_to_all(
        jnp.concatenate([send_rows, send_cots], axis=1),
        "expert",
        split_axis=0,
        concat_axis=0,
        tiled=True,
    )
    slots = expert_count * CAP
    shard = jnp.concatenate(
        [got[:, :CAP].reshape(slots, width), got[:, CAP:].reshape(slots, width)], axis=0
    )
    place, shard = lax.optimization_barrier((place, shard))
    gathered = lax.all_gather(shard, ("dp", "z", "core"), axis=0, tiled=True)
    gathered = gathered.reshape(dp_count, z_count * 2, 2, slots, width)
    packed = pack_columns(place, w_gate, w_up, w_down, z_count, width)
    other_cols = lax.ppermute(packed, "core", SWAP)
    mine = forward(gathered, w_gate, w_up, w_down)
    other = lax.ppermute(mine, "core", SWAP)
    far_out = out_terms(place, mine, other, w_down, other_cols, dp_count, (2,))
    far_back = back_terms(place, mine, other, w_gate, w_up, other_cols, dp_count, (2,))
    with jax.named_scope("hop1"):
        out_hop = first_hop(*far_out, "dp")
        back_hop = first_hop(*far_back, "z")
    rest, far_out, far_back = lax.optimization_barrier((place, far_out, far_back))
    out_rest = out_terms(rest, mine, other, w_down, other_cols, dp_count, (1, 3, 0))
    back_rest = back_terms(rest, mine, other, w_gate, w_up, other_cols, dp_count, (1, 3, 0))
    with jax.named_scope("hop2"):
        out_got = second_hop(out_hop, out_rest[0], out_rest[1], "dp")
        back_got = second_hop(back_hop, back_rest[0], back_rest[1], "z")
    acts, out_hop, back_hop = lax.optimization_barrier((mine, out_hop, back_hop))
    grads = weight_grads(acts, gathered)
    out_got, back_got, grads = lax.optimization_barrier((out_got, back_got, grads))
    grad_g, grad_u, grad_d = grads
    unsigned = [lax.axis_index(a).astype(jnp.uint32) for a in ("dp", "z")]
    out_at = picked(out_rest[2], out_got, unsigned[1])
    back_at = picked(back_rest[2], back_got, unsigned[0])
    half = jnp.bfloat16
    with jax.named_scope("hop3"):
        out_far, back_far = out_at(2).astype(half), back_at(2).astype(half)
        out_hop = first_hop(out_far[: slots // 2], out_far[slots // 2 :], "z")
        back_hop = first_hop(back_far[: slots // 2], back_far[slots // 2 :], "dp")
    with jax.named_scope("hop4"):
        out_got = second_hop(out_hop, out_at(1).astype(half), out_at(3).astype(half), "z")
        back_got = second_hop(back_hop, back_at(1).astype(half), back_at(3).astype(half), "dp")
    out_sum = (out_at(0) + wide(out_got[0]) + wide(out_got[1])).astype(half)
    back_sum = (back_at(0) + wide(back_got[0]) + wide(back_got[1])).astype(half)
    summed = jnp.concatenate([out_sum, back_sum], axis=1)
    summed = summed.reshape(expert_count, CAP, 2 * width)
    returned = lax.all_to_all(summed, "expert", split_axis=0, concat_axis=0, tiled=True)
    expert_out = returned[:, :, :width].astype(jnp.float32) * slot_gate[:, :, None]
    expert_back = returned[:, :, width:].astype(jnp.float32)
    mixed = jnp.einsum(
        "jct,jcf->tf", slot_table, expert_out, precision=lax.Precision.HIGHEST
    ).astype(jnp.bfloat16)
    grad_tokens = jnp.einsum(
        "jct,jcf->tf", slot_table, expert_back, precision=lax.Precision.HIGHEST
    ).astype(jnp.bfloat16)
    return (mixed, grad_tokens, grad_g, grad_u, grad_d)


def solution(mesh):
    dp, expert, tensor = (mesh.shape[a] for a in ("dp", "expert", "tensor"))
    fine = Mesh(mesh.devices.reshape(dp, expert, tensor // 2, 2), ("dp", "expert", "z", "core"))
    feats = P(("dp", "expert"), ("z", "core"))
    ids = P(("dp", "expert"), None)
    weights = P("expert", ("dp", "z", "core"), None)
    return jax.shard_map(
        on_device,
        mesh=fine,
        in_specs=(feats, feats, ids, ids, weights, weights, weights),
        out_specs=(feats, feats, weights, weights, weights),
        check_vma=False,
    )
```

```python
import jax
import jax.numpy as jnp
from jax import lax
from jax.experimental import pallas as pl
from jax.experimental.pallas import tpu as pltpu
from jax.sharding import Mesh
from jax.sharding import PartitionSpec as P

CAP = 48
VMEM_LIMIT = 48 * 1024 * 1024
PLANE = ("dp", "z")
SWAP = [(0, 1), (1, 0)]


def slot_tables(expert_ids, gate_fixed, expert_count):
    gate_value = gate_fixed.astype(jnp.float32) * (1.0 / 65536.0)
    matches = expert_ids[:, :, None] == jnp.arange(expert_count, dtype=jnp.int32)[None, None, :]
    chosen = jnp.any(matches, axis=1).astype(jnp.int32)
    weight = jnp.sum(jnp.where(matches, gate_value[:, :, None], 0.0), axis=1)
    slot_rank = jnp.cumsum(chosen, axis=0) - chosen
    in_slot = (slot_rank[:, :, None] == jnp.arange(CAP, dtype=jnp.int32)[None, None, :]) & (
        chosen[:, :, None] > 0
    )
    slot_table = jnp.transpose(in_slot.astype(jnp.float32), (1, 2, 0))
    slot_gate = jnp.einsum("jct,tj->jc", slot_table, weight, precision=lax.Precision.HIGHEST)
    return (slot_table, slot_gate)


def dot(a, b, dims):
    return lax.dot_general(a, b, (dims, ((), ())), preferred_element_type=jnp.float32)


def params(semantics=("arbitrary",)):
    return pltpu.CompilerParams(dimension_semantics=semantics, vmem_limit_bytes=VMEM_LIMIT)


def pack_columns(core, w_gate, w_up, w_down, z_count, width):
    hidden = w_gate.shape[1]

    def kernel(core_ref, g_ref, u_ref, d_ref, out_ref):
        out_ref[0, 0] = g_ref[0]
        out_ref[1, 0] = u_ref[0]
        out_ref[2, 0] = d_ref[0]

    spec = pl.BlockSpec((1, hidden, width), lambda z, core_ref: (0, 0, 2 * z + 1 - core_ref[0]))
    return pl.pallas_call(
        kernel,
        out_shape=jax.ShapeDtypeStruct((3, z_count, hidden, width), w_gate.dtype),
        grid_spec=pltpu.PrefetchScalarGridSpec(
            num_scalar_prefetch=1,
            grid=(z_count,),
            in_specs=[spec, spec, spec],
            out_specs=pl.BlockSpec((3, 1, hidden, width), lambda z, core_ref: (0, z, 0, 0)),
        ),
        compiler_params=params(),
        cost_estimate=pl.CostEstimate(
            flops=0, bytes_accessed=12 * z_count * hidden * width, transcendentals=0
        ),
        name="pack_columns",
    )(core, w_gate, w_up, w_down)


def forward(core, gathered, w_gate, w_up, w_down, other_cols):
    dp, z_count, _, slots, width = gathered.shape
    rows = dp * slots
    hidden = w_gate.shape[1]

    def kernel(core_ref, x_ref, g_ref, u_ref, d_ref, oc_ref, sum_ref, send_ref):
        z = pl.program_id(0)
        toks = x_ref[:, 0, 0].reshape(rows, width)
        cots = x_ref[:, 0, 1].reshape(rows, width)
        weights = (g_ref[0], u_ref[0], d_ref[0], oc_ref[0, 0], oc_ref[1, 0], oc_ref[2, 0])
        for k, w in enumerate(weights):
            part = dot(w, cots if k % 3 == 2 else toks, ((1,), (1,)))

            @pl.when(z == 0)
            def _(k=k, part=part):
                sum_ref[k] = part

            @pl.when(z > 0)
            def _(k=k, part=part):
                sum_ref[k] += part

        @pl.when(z == z_count - 1)
        def _():
            for k in range(6):
                send_ref[k] = sum_ref[k].astype(send_ref.dtype)

    cols = pl.BlockSpec((1, hidden, width), lambda z, core_ref: (0, 0, 2 * z + core_ref[0]))
    whole = pl.BlockSpec((6, hidden, rows), lambda z, core_ref: (0, 0, 0))
    return pl.pallas_call(
        kernel,
        out_shape=[
            jax.ShapeDtypeStruct((6, hidden, rows), jnp.float32),
            jax.ShapeDtypeStruct((6, hidden, rows), gathered.dtype),
        ],
        grid_spec=pltpu.PrefetchScalarGridSpec(
            num_scalar_prefetch=1,
            grid=(z_count,),
            in_specs=[
                pl.BlockSpec((dp, 1, 2, slots, width), lambda z, core_ref: (0, z, 0, 0, 0)),
                cols,
                cols,
                cols,
                pl.BlockSpec((3, 1, hidden, width), lambda z, core_ref: (0, z, 0, 0)),
            ],
            out_specs=[whole, whole],
        ),
        compiler_params=params(),
        cost_estimate=pl.CostEstimate(
            flops=12 * rows * hidden * width * z_count,
            bytes_accessed=(4 * rows + 12 * hidden) * width * z_count,
            transcendentals=0,
        ),
        name="forward",
    )(core, gathered, w_gate, w_up, w_down, other_cols)


def block_products(core, sums, got, w_gate, w_up, w_down, other_cols, dp):
    _, hidden, rows = sums.shape
    _, z_count, _, width = other_cols.shape
    slots = rows // dp
    half = other_cols.dtype

    def kernel(core_ref, s_ref, r_ref, g_ref, u_ref, d_ref, oc_ref, out_ref, act_ref, m_ref, o_ref):
        inner = ((1,), (0,))

        @pl.when(pl.program_id(0) == 0)
        def _():
            for at, turned in ((0, m_ref), (3, o_ref)):
                there = 3 - at
                gate = s_ref[at] + r_ref[there].astype(jnp.float32)
                up = s_ref[at + 1] + r_ref[there + 1].astype(jnp.float32)
                dhid = s_ref[at + 2] + r_ref[there + 2].astype(jnp.float32)
                sig = jax.nn.sigmoid(gate)
                acts = (
                    gate * sig * up,
                    dhid * up * sig * (1.0 + gate * (1.0 - sig)),
                    dhid * gate * sig,
                )
                for k, act in enumerate(acts):
                    act = act.astype(half)
                    act_ref[at + k] = act
                    turned[k] = act.T

        out = dot(m_ref[0], d_ref[0], inner) + dot(o_ref[0], oc_ref[2, 0], inner)
        out_ref[:, 0, :, :width] = out.astype(half).reshape(dp, slots, width)
        back = dot(m_ref[1], g_ref[0], inner) + dot(o_ref[1], oc_ref[0, 0], inner)
        back = back + dot(m_ref[2], u_ref[0], inner) + dot(o_ref[2], oc_ref[1, 0], inner)
        out_ref[:, 0, :, width:] = back.astype(half).reshape(dp, slots, width)

    whole = pl.BlockSpec((6, hidden, rows), lambda z, core_ref: (0, 0, 0))
    cols = pl.BlockSpec((1, hidden, width), lambda z, core_ref: (0, 0, 2 * z + core_ref[0]))
    return pl.pallas_call(
        kernel,
        out_shape=[
            jax.ShapeDtypeStruct((dp, z_count, slots, 2 * width), half),
            jax.ShapeDtypeStruct((6, hidden, rows), half),
        ],
        grid_spec=pltpu.PrefetchScalarGridSpec(
            num_scalar_prefetch=1,
            grid=(z_count,),
            in_specs=[
                whole,
                whole,
                cols,
                cols,
                cols,
                pl.BlockSpec((3, 1, hidden, width), lambda z, core_ref: (0, z, 0, 0)),
            ],
            out_specs=[
                pl.BlockSpec((dp, 1, slots, 2 * width), lambda z, core_ref: (0, z, 0, 0)),
                whole,
            ],
            scratch_shapes=[pltpu.VMEM((3, rows, hidden), half)] * 2,
        ),
        compiler_params=params(),
        cost_estimate=pl.CostEstimate(
            flops=12 * rows * hidden * width * z_count,
            bytes_accessed=(4 * rows + 12 * hidden) * width * z_count,
            transcendentals=2 * rows * hidden,
        ),
        name="block_products",
    )(core, sums, got, w_gate, w_up, w_down, other_cols)


def weight_grads(core, acts, gathered):
    dp, z_count, _, slots, width = gathered.shape
    _, hidden, rows = acts.shape

    def kernel(core_ref, a_ref, x_ref, g_ref, u_ref, d_ref, away_ref):
        toks = x_ref[:, 0, 0].reshape(rows, width)
        cots = x_ref[:, 0, 1].reshape(rows, width)
        inner = ((1,), (0,))
        g_ref[0] = dot(a_ref[1], toks, inner)
        u_ref[0] = dot(a_ref[2], toks, inner)
        d_ref[0] = dot(a_ref[0], cots, inner)
        away_ref[0, 0] = dot(a_ref[4], toks, inner)
        away_ref[1, 0] = dot(a_ref[5], toks, inner)
        away_ref[2, 0] = dot(a_ref[3], cots, inner)

    out = jax.ShapeDtypeStruct((1, hidden, 2 * z_count * width), jnp.float32)
    cols = pl.BlockSpec((1, hidden, width), lambda z, core_ref: (0, 0, 2 * z + core_ref[0]))
    return pl.pallas_call(
        kernel,
        out_shape=[out] * 3 + [jax.ShapeDtypeStruct((3, z_count, hidden, width), jnp.float32)],
        grid_spec=pltpu.PrefetchScalarGridSpec(
            num_scalar_prefetch=1,
            grid=(z_count,),
            in_specs=[
                pl.BlockSpec((6, hidden, rows), lambda z, core_ref: (0, 0, 0)),
                pl.BlockSpec((dp, 1, 2, slots, width), lambda z, core_ref: (0, z, 0, 0, 0)),
            ],
            out_specs=[cols] * 3
            + [pl.BlockSpec((3, 1, hidden, width), lambda z, core_ref: (0, z, 0, 0))],
        ),
        compiler_params=params(),
        cost_estimate=pl.CostEstimate(
            flops=12 * rows * hidden * width * z_count,
            bytes_accessed=(4 * rows + 24 * hidden) * width * z_count,
            transcendentals=0,
        ),
        name="weight_grads",
    )(core, acts, gathered)


def fill_columns(core, grads, got):
    _, z_count, hidden, width = got.shape

    def kernel(core_ref, got_ref, g_in, u_in, d_in, g_ref, u_ref, d_ref):
        g_ref[0] = got_ref[0, 0]
        u_ref[0] = got_ref[1, 0]
        d_ref[0] = got_ref[2, 0]

    cols = pl.BlockSpec((1, hidden, width), lambda z, core_ref: (0, 0, 2 * z + 1 - core_ref[0]))
    return pl.pallas_call(
        kernel,
        out_shape=[jax.ShapeDtypeStruct(g.shape, g.dtype) for g in grads],
        grid_spec=pltpu.PrefetchScalarGridSpec(
            num_scalar_prefetch=1,
            grid=(z_count,),
            in_specs=[pl.BlockSpec((3, 1, hidden, width), lambda z, core_ref: (0, z, 0, 0))]
            + [pl.BlockSpec(memory_space=pl.ANY)] * 3,
            out_specs=[cols] * 3,
        ),
        input_output_aliases={2: 0, 3: 1, 4: 2},
        compiler_params=params(),
        cost_estimate=pl.CostEstimate(
            flops=0, bytes_accessed=24 * z_count * hidden * width, transcendentals=0
        ),
        name="fill_columns",
    )(core, got, *grads)


def on_device(tokens, grad_out, expert_ids, gate_fixed, w_gate, w_up, w_down):
    expert_count = lax.axis_size("expert")
    dp_count = lax.axis_size("dp")
    z_count = lax.axis_size("z")
    width = tokens.shape[1]
    core = lax.axis_index("core").astype(jnp.int32).reshape(1)
    slot_table, slot_gate = slot_tables(expert_ids, gate_fixed, expert_count)
    table_half = slot_table.astype(jnp.bfloat16)
    send_rows = jnp.einsum(
        "jct,tf->jcf", table_half, tokens, preferred_element_type=jnp.float32
    ).astype(jnp.bfloat16)
    send_cots = jnp.einsum("jct,tf->jcf", table_half, grad_out, preferred_element_type=jnp.float32)
    send_cots = (send_cots * slot_gate[:, :, None]).astype(jnp.bfloat16)
    got = lax.all_to_all(
        jnp.concatenate([send_rows, send_cots], axis=1),
        "expert",
        split_axis=0,
        concat_axis=0,
        tiled=True,
    )
    slots = expert_count * CAP
    shard = jnp.concatenate(
        [got[:, :CAP].reshape(slots, width), got[:, CAP:].reshape(slots, width)], axis=0
    )
    core, shard = lax.optimization_barrier((core, shard))
    gathered = lax.all_gather(shard, PLANE, axis=0, tiled=True)
    gathered = gathered.reshape(dp_count, z_count, 2, slots, width)
    packed = pack_columns(core, w_gate, w_up, w_down, z_count, width)
    other_cols = lax.ppermute(packed, "core", SWAP)
    sums, sent = forward(core, gathered, w_gate, w_up, w_down, other_cols)
    got_sums = lax.ppermute(sent, "core", SWAP)
    terms, acts = block_products(
        core, sums, got_sums, w_gate, w_up, w_down, other_cols, dp_count
    )
    summed = lax.psum_scatter(
        terms.reshape(dp_count * z_count * slots, 2 * width),
        PLANE,
        scatter_dimension=0,
        tiled=True,
    )
    *grads, away = weight_grads(core, acts, gathered)
    grads = fill_columns(core, grads, lax.ppermute(away, "core", SWAP))
    summed, grads = lax.optimization_barrier((summed, grads))
    summed = summed.reshape(expert_count, CAP, 2 * width)
    returned = lax.all_to_all(summed, "expert", split_axis=0, concat_axis=0, tiled=True)
    expert_out = returned[:, :, :width].astype(jnp.float32) * slot_gate[:, :, None]
    expert_back = returned[:, :, width:].astype(jnp.float32)
    mixed = jnp.einsum(
        "jct,jcf->tf", slot_table, expert_out, precision=lax.Precision.HIGHEST
    ).astype(jnp.bfloat16)
    grad_tokens = jnp.einsum(
        "jct,jcf->tf", slot_table, expert_back, precision=lax.Precision.HIGHEST
    ).astype(jnp.bfloat16)
    return (mixed, grad_tokens, *grads)


def solution(mesh):
    dp, expert, tensor = (mesh.shape[a] for a in ("dp", "expert", "tensor"))
    fine = Mesh(mesh.devices.reshape(dp, expert, tensor // 2, 2), ("dp", "expert", "z", "core"))
    feats = P(("dp", "expert"), ("z", "core"))
    ids = P(("dp", "expert"), None)
    weights = P("expert", ("dp", "z", "core"), None)
    return jax.shard_map(
        on_device,
        mesh=fine,
        in_specs=(feats, feats, ids, ids, weights, weights, weights),
        out_specs=(feats, feats, weights, weights, weights),
        check_vma=False,
    )
```

```python
import jax
import jax.numpy as jnp
from jax import lax
from jax.experimental import pallas as pl
from jax.experimental.pallas import tpu as pltpu
from jax.sharding import Mesh
from jax.sharding import PartitionSpec as P

CAP = 48
VMEM_LIMIT = 61 * 1024 * 1024
RING = 4
PLANE = ("dp", "z")
SWAP = [(0, 1), (1, 0)]


def slot_tables(expert_ids, gate_fixed, expert_count):
    gate_value = gate_fixed.astype(jnp.float32) * (1.0 / 65536.0)
    matches = expert_ids[:, :, None] == jnp.arange(expert_count, dtype=jnp.int32)[None, None, :]
    chosen = jnp.any(matches, axis=1).astype(jnp.int32)
    weight = jnp.sum(jnp.where(matches, gate_value[:, :, None], 0.0), axis=1)
    slot_rank = jnp.cumsum(chosen, axis=0) - chosen
    in_slot = (slot_rank[:, :, None] == jnp.arange(CAP, dtype=jnp.int32)[None, None, :]) & (
        chosen[:, :, None] > 0
    )
    slot_table = jnp.transpose(in_slot.astype(jnp.float32), (1, 2, 0))
    slot_gate = jnp.einsum("jct,tj->jc", slot_table, weight, precision=lax.Precision.HIGHEST)
    return (slot_table, slot_gate)


def turned(index, by):
    return (index + by) & (RING - 1)


def dot(a, b, dims):
    return lax.dot_general(a, b, (dims, ((), ())), preferred_element_type=jnp.float32)


def params(semantics=("arbitrary",)):
    return pltpu.CompilerParams(dimension_semantics=semantics, vmem_limit_bytes=VMEM_LIMIT)


def pack_columns(place, w_gate, w_up, w_down, z_count, width):
    hidden = w_gate.shape[1]

    def kernel(core_ref, g_ref, u_ref, d_ref, out_ref):
        out_ref[0, 0] = g_ref[0]
        out_ref[1, 0] = u_ref[0]
        out_ref[2, 0] = d_ref[0]

    spec = pl.BlockSpec((1, hidden, width), lambda z, core_ref: (0, 0, 2 * z + 1 - core_ref[0]))
    return pl.pallas_call(
        kernel,
        out_shape=jax.ShapeDtypeStruct((3, z_count, hidden, width), w_gate.dtype),
        grid_spec=pltpu.PrefetchScalarGridSpec(
            num_scalar_prefetch=1,
            grid=(z_count,),
            in_specs=[spec, spec, spec],
            out_specs=pl.BlockSpec((3, 1, hidden, width), lambda z, core_ref: (0, z, 0, 0)),
        ),
        compiler_params=params(),
        cost_estimate=pl.CostEstimate(
            flops=0, bytes_accessed=12 * z_count * hidden * width, transcendentals=0
        ),
        name="pack_columns",
    )(place, w_gate, w_up, w_down)


def forward(gathered, w_gate, w_up, w_down):
    dp, tensor, _, slots, width = gathered.shape
    rows = dp * slots
    hidden = w_gate.shape[1]

    def kernel(x_ref, g_ref, u_ref, d_ref, out_ref, gate_acc, up_acc, dhid_acc):
        t = pl.program_id(0)
        toks = x_ref[:, 0, 0].reshape(rows, width)
        cots = x_ref[:, 0, 1].reshape(rows, width)
        last = ((1,), (1,))
        gate_part = dot(g_ref[0], toks, last)
        up_part = dot(u_ref[0], toks, last)
        dhid_part = dot(d_ref[0], cots, last)

        @pl.when(t == 0)
        def _():
            gate_acc[...] = gate_part
            up_acc[...] = up_part
            dhid_acc[...] = dhid_part

        @pl.when(t > 0)
        def _():
            gate_acc[...] += gate_part
            up_acc[...] += up_part
            dhid_acc[...] += dhid_part

        @pl.when(t == tensor - 1)
        def _():
            gate = gate_acc[...]
            up = up_acc[...]
            dhid = dhid_acc[...]
            sig = jax.nn.sigmoid(gate)
            out_ref[0] = (gate * sig * up).astype(out_ref.dtype)
            out_ref[1] = (dhid * up * sig * (1.0 + gate * (1.0 - sig))).astype(out_ref.dtype)
            out_ref[2] = (dhid * gate * sig).astype(out_ref.dtype)

    w_spec = pl.BlockSpec((1, hidden, width), lambda t: (0, 0, t))
    return pl.pallas_call(
        kernel,
        out_shape=jax.ShapeDtypeStruct((3, hidden, rows), gathered.dtype),
        grid=(tensor,),
        in_specs=[
            pl.BlockSpec((dp, 1, 2, slots, width), lambda t: (0, t, 0, 0, 0)),
            w_spec,
            w_spec,
            w_spec,
        ],
        out_specs=pl.BlockSpec((3, hidden, rows), lambda t: (0, 0, 0)),
        scratch_shapes=[pltpu.VMEM((hidden, rows), jnp.float32)] * 3,
        compiler_params=params(),
        cost_estimate=pl.CostEstimate(
            flops=6 * rows * hidden * width * tensor,
            bytes_accessed=(4 * rows + 6 * hidden) * width * tensor,
            transcendentals=rows * hidden,
        ),
        name="forward",
    )(gathered, w_gate, w_up, w_down)


def out_terms(place, mine, other, w_down, other_cols, dp):
    _, hidden, rows = mine.shape
    _, z_count, _, width = other_cols.shape
    slots = rows // dp

    def kernel(place_ref, mt_ref, ot_ref, d_ref, oc_ref, out_ref, m_ref, o_ref):
        @pl.when(pl.program_id(0) == 0)
        def _():
            m_ref[...] = mt_ref[0].T
            o_ref[...] = ot_ref[0].T

        inner = ((1,), (0,))
        out = dot(m_ref[...], d_ref[0], inner) + dot(o_ref[...], oc_ref[0, 0], inner)
        out_ref[:, 0] = out.astype(out_ref.dtype).reshape(dp, slots, width)

    acts = pl.BlockSpec((1, hidden, rows), lambda z, place_ref: (0, 0, 0))
    return pl.pallas_call(
        kernel,
        out_shape=jax.ShapeDtypeStruct((dp, z_count, slots, width), mine.dtype),
        grid_spec=pltpu.PrefetchScalarGridSpec(
            num_scalar_prefetch=1,
            grid=(z_count,),
            in_specs=[
                acts,
                acts,
                pl.BlockSpec((1, hidden, width), lambda z, place_ref: (0, 0, 2 * z + place_ref[0])),
                pl.BlockSpec((1, 1, hidden, width), lambda z, place_ref: (2, z, 0, 0)),
            ],
            out_specs=pl.BlockSpec((dp, 1, slots, width), lambda z, place_ref: (0, z, 0, 0)),
            scratch_shapes=[pltpu.VMEM((rows, hidden), mine.dtype)] * 2,
        ),
        compiler_params=params(),
        cost_estimate=pl.CostEstimate(
            flops=4 * rows * hidden * width * z_count,
            bytes_accessed=(2 * rows + 4 * hidden) * width * z_count,
            transcendentals=0,
        ),
        name="out_terms",
    )(place, mine, other, w_down, other_cols)


def back_terms(place, mine, other, w_gate, w_up, other_cols, dp, first, count):
    _, hidden, rows = mine.shape
    _, z_count, _, width = other_cols.shape
    slots = rows // dp
    def kernel(place_ref, mt_ref, ot_ref, g_ref, u_ref, oc_ref, *refs):
        *out_refs, m_ref, o_ref = refs
        j = pl.program_id(0)

        @pl.when(j == 0)
        def _():
            for k in range(2):
                m_ref[k] = mt_ref[k + 1].T
                o_ref[k] = ot_ref[k + 1].T

        inner = ((1,), (0,))
        back = dot(m_ref[0], g_ref[0], inner) + dot(o_ref[0], oc_ref[0, 0], inner)
        back = back + dot(m_ref[1], u_ref[0], inner) + dot(o_ref[1], oc_ref[1, 0], inner)
        back = back.astype(mine.dtype).reshape(dp, slots, width)
        if count == 1:
            out_refs[0][...] = back[: dp // 2]
            out_refs[1][...] = back[dp // 2 :]
        for k in range(count if count > 1 else 0):

            @pl.when(j == k)
            def _(k=k):
                out_refs[k][...] = back


    outs = [dp] * count if count > 1 else [dp // 2] * 2
    acts = pl.BlockSpec((3, hidden, rows), lambda j, place_ref: (0, 0, 0))
    cols = pl.BlockSpec(
        (1, hidden, width), lambda j, place_ref: (0, 0, 2 * place_ref[first + j] + place_ref[0])
    )
    return pl.pallas_call(
        kernel,
        out_shape=[jax.ShapeDtypeStruct((n, slots, width), mine.dtype) for n in outs],
        grid_spec=pltpu.PrefetchScalarGridSpec(
            num_scalar_prefetch=1,
            grid=(count,),
            in_specs=[
                acts,
                acts,
                cols,
                cols,
                pl.BlockSpec(
                    (2, 1, hidden, width), lambda j, place_ref: (0, place_ref[first + j], 0, 0)
                ),
            ],
            out_specs=[
                pl.BlockSpec((n, slots, width), lambda j, place_ref: (0, 0, 0)) for n in outs
            ],
            scratch_shapes=[pltpu.VMEM((2, rows, hidden), mine.dtype)] * 2,
        ),
        compiler_params=params(),
        cost_estimate=pl.CostEstimate(
            flops=8 * rows * hidden * width * count,
            bytes_accessed=(2 * rows + 8 * hidden) * width * count,
            transcendentals=0,
        ),
        name="back_terms",
    )(place, mine, other, w_gate, w_up, other_cols)


def wide(x):
    return x.astype(jnp.float32)


def around(axis, by):
    n = lax.axis_size(axis)
    return [(i, (i + by) % n) for i in range(n)]


def add_to_part(x, part, upper):
    free = x.shape[0] - part.shape[0]
    edges = [(free, 0) if upper else (0, free)] + [(0, 0)] * (x.ndim - 1)
    return (wide(x) + jnp.pad(wide(part), edges)).astype(x.dtype)


def first_hop(low, high, axis):
    return (
        lax.ppermute(low, axis, around(axis, 1)),
        lax.ppermute(high, axis, around(axis, -1)),
    )


def second_hop(passing, ahead, behind, axis):
    from_behind, from_ahead = passing
    return (
        lax.ppermute(add_to_part(ahead, from_behind, False), axis, around(axis, 1)),
        lax.ppermute(add_to_part(behind, from_ahead, True), axis, around(axis, -1)),
    )


def picked(own, got, place):
    def at(shift):
        def one(x):
            return wide(lax.dynamic_index_in_dim(x, turned(place, shift), 0, keepdims=False))

        return one(own) + one(got[0]) + one(got[1])

    return at


def weight_grads(acts_t, gathered):
    dp, tensor, _, slots, width = gathered.shape
    _, hidden, rows = acts_t.shape

    def kernel(a_ref, x_ref, g_ref, u_ref, d_ref):
        toks = x_ref[:, 0, 0].reshape(rows, width)
        cots = x_ref[:, 0, 1].reshape(rows, width)
        inner = ((1,), (0,))
        g_ref[0] = dot(a_ref[1], toks, inner)
        u_ref[0] = dot(a_ref[2], toks, inner)
        d_ref[0] = dot(a_ref[0], cots, inner)

    out = jax.ShapeDtypeStruct((1, hidden, tensor * width), jnp.float32)
    o_spec = pl.BlockSpec((1, hidden, width), lambda t: (0, 0, t))
    return pl.pallas_call(
        kernel,
        out_shape=(out, out, out),
        grid=(tensor,),
        in_specs=[
            pl.BlockSpec((3, hidden, rows), lambda t: (0, 0, 0)),
            pl.BlockSpec((dp, 1, 2, slots, width), lambda t: (0, t, 0, 0, 0)),
        ],
        out_specs=(o_spec, o_spec, o_spec),
        compiler_params=params(),
        cost_estimate=pl.CostEstimate(
            flops=6 * rows * hidden * width * tensor,
            bytes_accessed=(4 * rows + 12 * hidden) * width * tensor,
            transcendentals=0,
        ),
        name="weight_grads",
    )(acts_t, gathered)


def on_device(tokens, grad_out, expert_ids, gate_fixed, w_gate, w_up, w_down):
    expert_count = lax.axis_size("expert")
    dp_count = lax.axis_size("dp")
    z_count = lax.axis_size("z")
    width = tokens.shape[1]
    z_at = lax.axis_index("z").astype(jnp.int32)
    place = jnp.stack(
        [lax.axis_index("core").astype(jnp.int32)] + [turned(z_at, k) for k in (2, 1, 3, 0)]
    )
    slot_table, slot_gate = slot_tables(expert_ids, gate_fixed, expert_count)
    table_half = slot_table.astype(jnp.bfloat16)
    send_rows = jnp.einsum(
        "jct,tf->jcf", table_half, tokens, preferred_element_type=jnp.float32
    ).astype(jnp.bfloat16)
    send_cots = jnp.einsum("jct,tf->jcf", table_half, grad_out, preferred_element_type=jnp.float32)
    send_cots = (send_cots * slot_gate[:, :, None]).astype(jnp.bfloat16)
    got = lax.all_to_all(
        jnp.concatenate([send_rows, send_cots], axis=1),
        "expert",
        split_axis=0,
        concat_axis=0,
        tiled=True,
    )
    slots = expert_count * CAP
    shard = jnp.concatenate(
        [got[:, :CAP].reshape(slots, width), got[:, CAP:].reshape(slots, width)], axis=0
    )
    place, shard = lax.optimization_barrier((place, shard))
    gathered = lax.all_gather(shard, ("dp", "z", "core"), axis=0, tiled=True)
    gathered = gathered.reshape(dp_count, z_count * 2, 2, slots, width)
    packed = pack_columns(place, w_gate, w_up, w_down, z_count, width)
    other_cols = lax.ppermute(packed, "core", SWAP)
    mine = forward(gathered, w_gate, w_up, w_down)
    other = lax.ppermute(mine, "core", SWAP)
    half = jnp.bfloat16
    outs = out_terms(place, mine, other, w_down, other_cols, dp_count)
    out_sum = lax.psum_scatter(
        outs.reshape(dp_count * z_count * slots, width), PLANE, scatter_dimension=0, tiled=True
    )
    next_place, outs = lax.optimization_barrier((place, outs))
    far_back = back_terms(next_place, mine, other, w_gate, w_up, other_cols, dp_count, 1, 1)
    back_hop = first_hop(*far_back, "z")
    rest, far_back = lax.optimization_barrier((next_place, far_back))
    back_rest = back_terms(rest, mine, other, w_gate, w_up, other_cols, dp_count, 2, 3)
    back_got = second_hop(back_hop, back_rest[0], back_rest[1], "z")
    acts, back_hop = lax.optimization_barrier((mine, back_hop))
    grads = weight_grads(acts, gathered)
    back_got, grads = lax.optimization_barrier((back_got, grads))
    grad_g, grad_u, grad_d = grads
    back_at = picked(back_rest[2], back_got, lax.axis_index("dp").astype(jnp.uint32))
    back_far = back_at(2).astype(half)
    back_hop = first_hop(back_far[: slots // 2], back_far[slots // 2 :], "dp")
    back_got = second_hop(back_hop, back_at(1).astype(half), back_at(3).astype(half), "dp")
    back_sum = (back_at(0) + wide(back_got[0]) + wide(back_got[1])).astype(half)
    out_sum, back_sum = lax.optimization_barrier((out_sum, back_sum))
    summed = jnp.concatenate([out_sum, back_sum], axis=1)
    summed = summed.reshape(expert_count, CAP, 2 * width)
    returned = lax.all_to_all(summed, "expert", split_axis=0, concat_axis=0, tiled=True)
    expert_out = returned[:, :, :width].astype(jnp.float32) * slot_gate[:, :, None]
    expert_back = returned[:, :, width:].astype(jnp.float32)
    mixed = jnp.einsum(
        "jct,jcf->tf", slot_table, expert_out, precision=lax.Precision.HIGHEST
    ).astype(jnp.bfloat16)
    grad_tokens = jnp.einsum(
        "jct,jcf->tf", slot_table, expert_back, precision=lax.Precision.HIGHEST
    ).astype(jnp.bfloat16)
    return (mixed, grad_tokens, grad_g, grad_u, grad_d)


def solution(mesh):
    dp, expert, tensor = (mesh.shape[a] for a in ("dp", "expert", "tensor"))
    fine = Mesh(mesh.devices.reshape(dp, expert, tensor // 2, 2), ("dp", "expert", "z", "core"))
    feats = P(("dp", "expert"), ("z", "core"))
    ids = P(("dp", "expert"), None)
    weights = P("expert", ("dp", "z", "core"), None)
    return jax.shard_map(
        on_device,
        mesh=fine,
        in_specs=(feats, feats, ids, ids, weights, weights, weights),
        out_specs=(feats, feats, weights, weights, weights),
        check_vma=False,
    )
```
